256 devices in a mesh: dp: 2 (over z_lo), seq: 32 (over y, x, core), head: 4 (over z_hi).
Axes of the slice: x: 4, y: 4, z: 8 (z_hi: 4, z_lo: 2; z = z_hi * 2 + z_lo), core: 2. Of those that a mesh axis runs over, the one named last changes fastest.
Arguments:
- x_in: bfloat16 [2, 24576, 4096], P('dp', 'seq', 'head'), may hold values from -6 to 6
- b_in: bfloat16 [2, 24576, 1024], P('dp', 'seq', 'head'), may hold values from -6 to 6
- c_in: bfloat16 [2, 24576, 1024], P('dp', 'seq', 'head'), may hold values from -6 to 6
- z_in: bfloat16 [2, 24576, 4096], P('dp', 'seq', 'head'), may hold values from -24 to 24
- dt_in: float32 [2, 64, 24576], P('dp', 'head', 'seq'), may hold values from -10 to 4.5
- a_log: float32 [64], P('head'), may hold values from -2.3 to 0.58
- skip_gain: float32 [64], P('head'), may hold values from 0.5 to 1.5
- norm_gain: float32 [4096], P('head'), may hold values from 0.5 to 1.5
- conv_x: float32 [4, 4096], P(None, 'head'), may hold values from -3 to 3
- conv_b: float32 [4, 1024], P(None, 'head'), may hold values from -3 to 3
- conv_c: float32 [4, 1024], P(None, 'head'), may hold values from -3 to 3
- init_state: float32 [2, 64, 64, 128], P('dp', 'head'), may hold values from -0.5 to 0.5
- out_weight: bfloat16 [4096, 8192], P(('dp', 'seq'), 'head'), may hold values from -0.09375 to 0.09375
Outputs:
- mixed: bfloat16 [2, 24576, 8192], P('dp', 'seq', 'head')
The draws below stay inside these ranges and needn't reach their ends.
All inputs are finite; a program needn't handle non-finite values.
Results may differ from the reference program's by a relative error of at most 0.0058.
Values may be sent and summed in bfloat16 or wider, within the bound.
No kernel may reach another device: no remote copies, remote signals or barrier semaphores. Data moves between devices by JAX's collectives and lax.ppermute only.
A program may use at most 128 MiB of HBM per device.

```python
import math
import jax
import jax.numpy as jnp
from jax import lax

D = 8192
HEAD_SIZE = 64
STATE = 128
BLOCK_LEN = 256
TAPS = 4
TOK_DEV = 768
SSM_HEAD_COUNT = 64
GROUPS = 8
SEQ_LEN = 24576
ROLLOUT_COUNT = 2


def fast_heads(key):
    chooser = jax.random.fold_in(key, 101)
    fast_share = 0.5
    return jax.random.uniform(chooser, (SSM_HEAD_COUNT,)) < fast_share


def head_log_rates(key):
    fast_mask = fast_heads(key)
    jitter = jax.random.uniform(jax.random.fold_in(key, 202), (SSM_HEAD_COUNT,), jnp.float32, -0.35, 0.35)
    slow_level = jax.random.uniform(jax.random.fold_in(key, 212), (SSM_HEAD_COUNT,), jnp.float32, -2.3, -1.6)
    return jnp.where(fast_mask, math.log(1.25) + jitter, slow_level).astype(jnp.float32)


def draw_a_log(key, part):
    return head_log_rates(key)


def draw_dt_in(key, part):
    fast_mask = fast_heads(key)[None, :, None]
    rates = jnp.exp(head_log_rates(key))[None, :, None]
    blocks = SEQ_LEN // TOK_DEV
    jitter_tok = jax.random.uniform(jax.random.fold_in(key, 303), (ROLLOUT_COUNT, SSM_HEAD_COUNT, blocks, TOK_DEV), jnp.float32, -0.7, 0.7)
    offset = jax.random.uniform(jax.random.fold_in(key, 404), (ROLLOUT_COUNT, SSM_HEAD_COUNT, blocks, 1), jnp.float32, -0.4, 0.4)
    noisy_portion = (jitter_tok + offset).reshape(ROLLOUT_COUNT, SSM_HEAD_COUNT, SEQ_LEN)
    target = jax.random.uniform(jax.random.fold_in(key, 313), (ROLLOUT_COUNT, SSM_HEAD_COUNT, 1), jnp.float32, 1.0, 1.5)
    slow_level = jnp.log(target / (SEQ_LEN * rates))
    baseline_level = jnp.where(fast_mask, math.log(0.02), slow_level)
    location_list = jax.random.randint(jax.random.fold_in(key, 505), (ROLLOUT_COUNT, 2), 0, SEQ_LEN)
    token_position = jnp.arange(SEQ_LEN)
    spike_mask = jnp.any(token_position[None, None, :] == location_list[:, :, None], axis=1)[:, None, :]
    loss_share = jax.random.uniform(jax.random.fold_in(key, 606), (ROLLOUT_COUNT, SSM_HEAD_COUNT, 1), jnp.float32, 0.2, 0.35)
    spike_step = -jnp.log1p(-loss_share) / rates
    spike_value = jnp.log(jnp.expm1(spike_step))
    return jnp.where(spike_mask, spike_value, baseline_level + noisy_portion).astype(jnp.float32)


def draw_z_in(key, part):
    shape_full = (ROLLOUT_COUNT, SEQ_LEN, SSM_HEAD_COUNT * HEAD_SIZE)
    column = jnp.exp(jax.random.uniform(jax.random.fold_in(key, 707), (SSM_HEAD_COUNT * HEAD_SIZE,), jnp.float32, math.log(0.3), math.log(3.0)))
    row_scale = jnp.exp(jax.random.uniform(jax.random.fold_in(key, 808), (ROLLOUT_COUNT, SEQ_LEN, 1), jnp.float32, math.log(0.5), math.log(2.0)))
    values = jax.random.truncated_normal(jax.random.fold_in(key, 909), -4.0, 4.0, shape_full, jnp.float32)
    return (values * column * row_scale).astype(jnp.bfloat16)


def steps_of(key, shape, split, low, largest):
    factor_of, own = 1.0, jax.random.fold_in(key, 6)
    for dim, parts in split:
        steps = jnp.exp(jax.random.uniform(jax.random.fold_in(own, dim), (parts,), jnp.float32, low / len(split), largest / len(split)))
        factor_of = factor_of * jnp.repeat(steps, shape[dim] // parts).reshape([-1 if axis == dim else 1 for axis in range(len(shape))])
    return factor_of


def gaussian(own_key, shape, scale, bound, pieces=(), dtype=jnp.bfloat16):
    loudness = steps_of(own_key, shape, pieces, -0.22, 0.18) if pieces else 1.0
    result = jax.random.normal(own_key, shape, jnp.float32) * scale * loudness
    return jnp.minimum(jnp.maximum(result, -bound), bound).astype(dtype)


def setup_inputs(seed: int = 0) -> dict:
    streams_of = jax.random.split(jax.random.key(seed), 14)
    x_in = gaussian(streams_of[0], (ROLLOUT_COUNT, SEQ_LEN, SSM_HEAD_COUNT * HEAD_SIZE), 1.0, 6.0, ((0, 2), (1, 32), (2, 4)))
    b_in = gaussian(streams_of[1], (ROLLOUT_COUNT, SEQ_LEN, GROUPS * STATE), 1.0, 6.0, ((0, 2), (1, 32), (2, 4)))
    c_in = gaussian(streams_of[2], (ROLLOUT_COUNT, SEQ_LEN, GROUPS * STATE), 1.0, 6.0, ((0, 2), (1, 32), (2, 4)))
    z_in = draw_z_in(jax.random.fold_in(streams_of[13], 71), 0)
    dt_in = draw_dt_in(jax.random.fold_in(streams_of[13], 71), 0)
    a_log = draw_a_log(jax.random.fold_in(streams_of[13], 71), 0)
    skip_gain = jnp.clip(0.5 + 1.0 * jax.random.uniform(streams_of[6], (SSM_HEAD_COUNT,), jnp.float32) ** steps_of(streams_of[6], (SSM_HEAD_COUNT,), ((0, 4),), -0.2, 0.2), 0.5, 1.5)
    norm_gain = jnp.clip(1.0 + 0.1 * jax.random.normal(streams_of[7], (SSM_HEAD_COUNT * HEAD_SIZE,), jnp.float32), 0.5, 1.5)
    conv_x = gaussian(streams_of[8], (TAPS, SSM_HEAD_COUNT * HEAD_SIZE), TAPS ** -0.5, 3.0, ((1, 4),), jnp.float32)
    conv_b = gaussian(streams_of[9], (TAPS, GROUPS * STATE), TAPS ** -0.5, 3.0, ((1, 4),), jnp.float32)
    conv_c = gaussian(streams_of[10], (TAPS, GROUPS * STATE), TAPS ** -0.5, 3.0, ((1, 4),), jnp.float32)
    init_state = gaussian(streams_of[11], (ROLLOUT_COUNT, SSM_HEAD_COUNT, HEAD_SIZE, STATE), 0.08, 0.5, ((0, 2), (1, 4)), jnp.float32)
    out_weight = gaussian(streams_of[12], (SSM_HEAD_COUNT * HEAD_SIZE, D), (SSM_HEAD_COUNT * HEAD_SIZE) ** -0.5, 0.09375, ((0, 64), (1, 4)))
    return {"x_in": x_in, "b_in": b_in, "c_in": c_in, "z_in": z_in, "dt_in": dt_in, "a_log": a_log, "skip_gain": skip_gain, "norm_gain": norm_gain, "conv_x": conv_x, "conv_b": conv_b, "conv_c": conv_c, "init_state": init_state, "out_weight": out_weight}


EPSILON = 1e-05

def causal_conv(signal, before, weight):
    joined = jnp.concatenate([before, signal], axis=1).astype(jnp.float32)
    length = signal.shape[1]
    tap_count = weight.shape[0]
    accum_total = weight[0] * joined[:, 0:length]
    for offset in range(1, tap_count):
        accum_total = accum_total + weight[offset] * joined[:, offset:offset + length]
    return jax.nn.silu(accum_total).astype(jnp.bfloat16)

def to_narrow(value):
    return lax.optimization_barrier(value.astype(jnp.bfloat16)).astype(jnp.float32)

def reference(x_in, b_in, c_in, z_in, dt_in, a_log, skip_gain, norm_gain, conv_x, conv_b, conv_c, init_state, out_weight):
    highest = lax.Precision.HIGHEST
    rim_width = TAPS - 1
    roll_count = x_in.shape[0]
    x_conv = causal_conv(x_in, jnp.zeros((roll_count, rim_width, x_in.shape[2]), jnp.bfloat16), conv_x)
    b_conv = causal_conv(b_in, jnp.zeros((roll_count, rim_width, b_in.shape[2]), jnp.bfloat16), conv_b)
    c_conv = causal_conv(c_in, jnp.zeros((roll_count, rim_width, c_in.shape[2]), jnp.bfloat16), conv_c)
    per_group = SSM_HEAD_COUNT // GROUPS
    block_count = SEQ_LEN // BLOCK_LEN
    step_size = jax.nn.softplus(dt_in)
    log_decay = step_size * (-jnp.exp(a_log))[None, :, None]

    def to_blocks(data, inner):
        return jnp.moveaxis(data.reshape((roll_count, block_count, BLOCK_LEN) + inner), 1, 0)
    x_blocks = to_blocks(x_conv, (GROUPS, per_group, HEAD_SIZE))
    b_blocks = to_blocks(b_conv, (GROUPS, STATE))
    c_blocks = to_blocks(c_conv, (GROUPS, STATE))
    dt_blocks = jnp.moveaxis(step_size.reshape(roll_count, GROUPS, per_group, block_count, BLOCK_LEN), 3, 0)
    decay_blocks = jnp.moveaxis(log_decay.reshape(roll_count, GROUPS, per_group, block_count, BLOCK_LEN), 3, 0)
    skip_shaped = skip_gain.reshape(GROUPS, per_group)[:, :, None]
    query_pos = lax.broadcasted_iota(jnp.int32, (BLOCK_LEN, BLOCK_LEN), 0)
    key_pos = lax.broadcasted_iota(jnp.int32, (BLOCK_LEN, BLOCK_LEN), 1)
    causal = query_pos >= key_pos

    def advance(state, inputs):
        x_block, b_block, c_block, dt_block, decay_block = inputs
        x_float = x_block.astype(jnp.float32)
        b_float = b_block.astype(jnp.float32)
        c_float = c_block.astype(jnp.float32)
        cum_decay = jnp.cumsum(decay_block, axis=-1)
        scores = jnp.einsum('rqgn,rsgn->rgqs', c_float, b_float, precision=highest)
        spread = cum_decay[..., :, None] - cum_decay[..., None, :]
        decay_mat = jnp.where(causal, jnp.exp(jnp.minimum(spread, 0.0)), jnp.float32(0.0))
        mixing = to_narrow(scores[:, :, None] * decay_mat * dt_block[..., None, :])
        intra_out = jnp.einsum('rgkqs,rsgkp->rqgkp', mixing, x_float, precision=highest)
        inter_out = jnp.einsum('rqgn,rgkpn->rqgkp', c_float, state, precision=highest)
        inter_out = inter_out * jnp.transpose(jnp.exp(cum_decay), (0, 3, 1, 2))[..., None]
        last_decay = cum_decay[..., -1:]
        weights_in = jnp.exp(last_decay - cum_decay) * dt_block
        weighted = to_narrow(jnp.transpose(weights_in, (0, 3, 1, 2))[..., None] * x_float)
        fresh = jnp.einsum('rsgkp,rsgn->rgkpn', weighted, b_float, precision=highest)
        new_state = jnp.exp(last_decay)[..., None] * state + fresh
        return (new_state, intra_out + inter_out + skip_shaped * x_float)
    start_state = init_state.reshape(roll_count, GROUPS, per_group, HEAD_SIZE, STATE)
    final_state, outputs = lax.scan(advance, start_state, (x_blocks, b_blocks, c_blocks, dt_blocks, decay_blocks))
    ssm_out = jnp.moveaxis(outputs, 0, 1).reshape(roll_count, SEQ_LEN, GROUPS, per_group * HEAD_SIZE)
    gate_act = jax.nn.silu(z_in.astype(jnp.float32)).reshape(roll_count, SEQ_LEN, GROUPS, per_group * HEAD_SIZE)
    gated_out = ssm_out * gate_act
    mean_sq = lax.optimization_barrier(jnp.mean(gated_out * gated_out, axis=-1, keepdims=True))
    normed = gated_out * lax.rsqrt(mean_sq + EPSILON) * norm_gain.reshape(GROUPS, per_group * HEAD_SIZE)
    normed = normed.astype(jnp.bfloat16).reshape(roll_count, SEQ_LEN, SSM_HEAD_COUNT * HEAD_SIZE)

    def project_roll(normed_roll):
        return jnp.dot(normed_roll, out_weight, preferred_element_type=jnp.float32).astype(jnp.bfloat16)
    return lax.map(project_roll, normed)
```

```python
import math

import jax
import jax.numpy as jnp
from jax import lax
from jax.experimental import pallas as pl
from jax.experimental.pallas import tpu as pltpu
from jax.sharding import PartitionSpec as P

HEAD_SIZE = 64
STATE = 128
TAPS = 4
SUB = 128
CHUNK = 256
EPSILON = 1e-05
LOG2E = math.log2(math.e)
F32 = jnp.float32
BF16 = jnp.bfloat16


def dot(a, b, dims=((1,), (0,))):
    return lax.dot_general(a, b, (dims, ((), ())), preferred_element_type=F32)


def silu(v):
    half = 0.5 * v
    return half + half * jnp.tanh(half)


def split_two(v):
    high = v.astype(BF16)
    low = (v - high.astype(F32)).astype(BF16)
    return high, low


def head_of_lane(heads, width):
    lane = lax.broadcasted_iota(jnp.int32, (heads, width), 1)
    row = lax.broadcasted_iota(jnp.int32, (heads, width), 0)
    return lane // HEAD_SIZE == row


def widen_row(column, width):
    mask = head_of_lane(column.shape[0], width)
    return jnp.sum(jnp.where(mask, column, 0.0), axis=0, keepdims=True)


def column_of(ref, heads):
    row = lax.broadcasted_iota(jnp.int32, (heads, 1), 0)
    column = jnp.zeros((heads, 1), F32)
    for h in range(heads):
        column = jnp.where(row == h, ref[h], column)
    return column


def widen_tokens(rows, width):
    heads = rows.shape[0]
    mask = head_of_lane(heads, width).astype(F32).astype(BF16)
    high, low = split_two(rows)
    return dot(
        jnp.concatenate([high, low], axis=0), jnp.concatenate([mask, mask], axis=0), ((0,), (0,))
    )


def edge_kernel(x_ref, b_ref, c_ref, out_ref):
    wide_x, wide_b = x_ref.shape[1], b_ref.shape[1]
    out_ref[:, :wide_x] = x_ref[...]
    out_ref[:, wide_x : wide_x + wide_b] = b_ref[...]
    out_ref[:, wide_x + wide_b :] = c_ref[...]


def edge_rows(x, b, c):
    tokens, wide_x = x.shape
    wide_b = b.shape[1]
    last = tokens // 8 - 1
    return pl.pallas_call(
        edge_kernel,
        grid=(1,),
        in_specs=[
            pl.BlockSpec((8, wide_x), lambda i: (last, 0)),
            pl.BlockSpec((8, wide_b), lambda i: (last, 0)),
            pl.BlockSpec((8, wide_b), lambda i: (last, 0)),
        ],
        out_specs=pl.BlockSpec((8, wide_x + 2 * wide_b), lambda i: (0, 0)),
        out_shape=jax.ShapeDtypeStruct((8, wide_x + 2 * wide_b), BF16),
        name="edge",
    )(x, b, c)


def conv_into(raw_ref, tail_ref, weight_ref, lo, pad_ref, out_ref):
    rows, width = raw_ref.shape
    raw = raw_ref[...].astype(F32)
    pad_ref[0:8, lo : lo + width] = tail_ref[:, lo : lo + width]
    pad_ref[8 : 8 + rows, lo : lo + width] = raw
    tail_ref[:, lo : lo + width] = raw[rows - 8 :]
    total = weight_ref[TAPS - 1 : TAPS, :] * raw
    for back in range(1, TAPS):
        tap = TAPS - 1 - back
        total = total + weight_ref[tap : tap + 1, :] * pad_ref[8 - back : 8 - back + rows, lo : lo + width]
    out_ref[...] = silu(total).astype(BF16)


def front_kernel(
    first_ref,
    x_ref,
    b_ref,
    c_ref,
    halo_ref,
    dt_ref,
    alog_ref,
    cx_ref,
    cb_ref,
    cc_ref,
    init_ref,
    xo_ref,
    bo_ref,
    co_ref,
    cum_ref,
    key_ref,
    fresh_ref,
    drop_ref,
    start_ref,
    msg_ref,
    pad_ref,
    tail_ref,
    weight_ref,
    state_ref,
):
    step = pl.program_id(0)
    wide_x, wide_b = x_ref.shape[1], b_ref.shape[1]
    heads, tokens = dt_ref.shape
    subs = tokens // SUB
    groups = wide_b // STATE
    lanes = wide_x // groups

    @pl.when(step == 0)
    def _():
        tail_ref[...] = halo_ref[...].astype(F32)
        raw = dt_ref[...]
        grown = jnp.exp(-jnp.abs(raw))
        near = 1.0 + grown
        gap = near - 1.0
        log_near = jnp.where(gap == 0.0, grown, jnp.log(near) * grown / jnp.where(gap == 0.0, 1.0, gap))
        size = jnp.maximum(raw, 0.0) + log_near
        rate = size * (-LOG2E * jnp.exp(column_of(alog_ref, heads)))
        lane = lax.broadcasted_iota(jnp.int32, (heads, SUB), 1)
        rows = []
        for j in range(subs):
            cum = rate[:, j * SUB : (j + 1) * SUB]
            shift = 1
            while shift < SUB:
                cum = cum + jnp.where(lane >= shift, pltpu.roll(cum, shift, 1), 0.0)
                shift *= 2
            size_j = size[:, j * SUB : (j + 1) * SUB]
            last = cum[:, SUB - 1 : SUB]
            cum_ref[:, j * SUB : (j + 1) * SUB] = cum
            key_ref[:, j * SUB : (j + 1) * SUB] = cum - jnp.log(size_j) * LOG2E
            weight_ref[:, j * SUB : (j + 1) * SUB] = jnp.exp2(last - cum) * size_j
            rows.append(widen_row(jnp.exp2(last), wide_x))
        rows += [jnp.ones((1, wide_x), F32)] * (8 - subs)
        drop_ref[...] = jnp.concatenate(rows, axis=0)

        @pl.when(first_ref[0] == 1)
        def _():
            for k in range(wide_x // STATE):
                state_ref[:, k * STATE : (k + 1) * STATE] = init_ref[k * STATE : (k + 1) * STATE, :].T

        @pl.when(first_ref[0] != 1)
        def _():
            state_ref[...] = jnp.zeros_like(state_ref)

        start_ref[...] = state_ref[...]

    conv_into(x_ref, tail_ref, cx_ref, 0, pad_ref, xo_ref)
    conv_into(b_ref, tail_ref, cb_ref, wide_x, pad_ref, bo_ref)
    conv_into(c_ref, tail_ref, cc_ref, wide_x + wide_b, pad_ref, co_ref)

    per_step = x_ref.shape[0] // SUB
    for k in range(per_step):
        at = pl.multiple_of(step * (per_step * SUB) + k * SUB, SUB)
        spread = widen_tokens(weight_ref[:, pl.ds(at, SUB)], wide_x)
        inner = (spread * xo_ref[k * SUB : (k + 1) * SUB, :].astype(F32)).astype(BF16)
        fall = drop_ref[pl.ds(step * per_step + k, 1), :]
        for g in range(groups):
            fresh = dot(
                bo_ref[k * SUB : (k + 1) * SUB, g * STATE : (g + 1) * STATE],
                inner[:, g * lanes : (g + 1) * lanes],
                ((0,), (0,)),
            )
            fresh_ref[k, :, g * lanes : (g + 1) * lanes] = fresh
            state_ref[:, g * lanes : (g + 1) * lanes] = (
                fall[:, g * lanes : (g + 1) * lanes] * state_ref[:, g * lanes : (g + 1) * lanes] + fresh
            )

    @pl.when(step == pl.num_programs(0) - 1)
    def _():
        tiles = STATE // 8
        whole = drop_ref[0:1, :]
        for j in range(1, subs):
            whole = whole * drop_ref[j : j + 1, :]
        high = whole.astype(BF16).astype(F32)
        low = whole - high
        for g in range(groups):
            own = state_ref[:, g * lanes : (g + 1) * lanes].reshape(tiles, 8, lanes)
            msg_ref[g * tiles : (g + 1) * tiles, :, :lanes] = own.astype(BF16)
            pieces = [
                part[:, g * lanes + q * 128 : g * lanes + (q + 1) * 128]
                for part in (high, low)
                for q in range(lanes // 128)
            ]
            tile = jnp.concatenate(pieces, axis=0)
            msg_ref[g * tiles : (g + 1) * tiles, :, lanes:] = jnp.broadcast_to(
                tile[None], (tiles, 8, 128)
            ).astype(BF16)


def front(first, x, b, c, halo, dt, a_log, conv_x, conv_b, conv_c, init):
    tokens, wide_x = x.shape
    wide_b = b.shape[1]
    heads = dt.shape[0]
    subs = tokens // SUB
    groups = wide_b // STATE
    lanes = wide_x // groups
    parts = groups * STATE // 8
    per_step = CHUNK // SUB

    def whole(*shape):
        return pl.BlockSpec(shape, lambda i, *_: (0,) * len(shape))

    return pl.pallas_call(
        front_kernel,
        grid_spec=pltpu.PrefetchScalarGridSpec(
            num_scalar_prefetch=1,
            grid=(tokens // CHUNK,),
            in_specs=[
                pl.BlockSpec((CHUNK, wide_x), lambda i, *_: (i, 0)),
                pl.BlockSpec((CHUNK, wide_b), lambda i, *_: (i, 0)),
                pl.BlockSpec((CHUNK, wide_b), lambda i, *_: (i, 0)),
                whole(8, wide_x + 2 * wide_b),
                whole(heads, tokens),
                pl.BlockSpec(memory_space=pltpu.SMEM),
                whole(TAPS, wide_x),
                whole(TAPS, wide_b),
                whole(TAPS, wide_b),
                whole(wide_x, STATE),
            ],
            out_specs=[
                pl.BlockSpec((CHUNK, wide_x), lambda i, *_: (i, 0)),
                pl.BlockSpec((CHUNK, wide_b), lambda i, *_: (i, 0)),
                pl.BlockSpec((CHUNK, wide_b), lambda i, *_: (i, 0)),
                whole(heads, tokens),
                whole(heads, tokens),
                pl.BlockSpec((per_step, STATE, wide_x), lambda i, *_: (i, 0, 0)),
                whole(8, wide_x),
                whole(STATE, wide_x),
                whole(parts, 8, lanes + 128),
            ],
            scratch_shapes=[
                pltpu.VMEM((CHUNK + 8, wide_x + 2 * wide_b), F32),
                pltpu.VMEM((8, wide_x + 2 * wide_b), F32),
                pltpu.VMEM((heads, tokens), F32),
                pltpu.VMEM((STATE, wide_x), F32),
            ],
        ),
        out_shape=[
            jax.ShapeDtypeStruct((tokens, wide_x), BF16),
            jax.ShapeDtypeStruct((tokens, wide_b), BF16),
            jax.ShapeDtypeStruct((tokens, wide_b), BF16),
            jax.ShapeDtypeStruct((heads, tokens), F32),
            jax.ShapeDtypeStruct((heads, tokens), F32),
            jax.ShapeDtypeStruct((subs, STATE, wide_x), F32),
            jax.ShapeDtypeStruct((8, wide_x), F32),
            jax.ShapeDtypeStruct((STATE, wide_x), F32),
            jax.ShapeDtypeStruct((parts, 8, lanes + 128), BF16),
        ],
        name="front",
    )(first, x, b, c, halo, dt, a_log, conv_x, conv_b, conv_c, init)


def scan_kernel(msg_ref, out_ref):
    slabs, _, wide = msg_ref.shape
    lanes = wide - 128
    pieces = lanes // 128
    running = [jnp.zeros((8, 128), F32) for _ in range(pieces)]
    for s in range(slabs):
        falls = msg_ref[s, :, lanes:].astype(F32)
        for q in range(pieces):
            out_ref[s, :, q * 128 : (q + 1) * 128] = running[q].astype(BF16)
            fall = falls[q : q + 1, :] + falls[pieces + q : pieces + q + 1, :]
            running[q] = fall * running[q] + msg_ref[s, :, q * 128 : (q + 1) * 128].astype(F32)


def scan_slabs(msg):
    slabs, _, wide = msg.shape
    return pl.pallas_call(
        scan_kernel,
        out_shape=jax.ShapeDtypeStruct((slabs, 8, wide - 128), BF16),
        name="scan",
    )(msg)


def chunk_kernel(
    x_ref,
    b_ref,
    c_ref,
    z_ref,
    cum_ref,
    key_ref,
    fresh_ref,
    drop_ref,
    skip_ref,
    gain_ref,
    came_ref,
    start_ref,
    top_ref,
    bottom_ref,
    next_ref,
    state_ref,
    *,
    base,
):
    step = pl.program_id(0)
    wide_x, wide_b = x_ref.shape[1], b_ref.shape[1]
    groups = wide_b // STATE
    lanes = wide_x // groups
    heads = cum_ref.shape[0]
    per_group = heads // groups

    @pl.when(step == 0)
    def _():
        if base == 0:
            tiles = STATE // 8
            for g in range(groups):
                came = came_ref[g * tiles : (g + 1) * tiles].astype(F32).reshape(STATE, lanes)
                state_ref[:, g * lanes : (g + 1) * lanes] = (
                    came + start_ref[:, g * lanes : (g + 1) * lanes]
                )
        else:
            state_ref[...] = came_ref[...]

    cum = cum_ref[...]
    cum_cols = cum.T
    spread = widen_tokens(jnp.exp2(cum), wide_x)
    fall = drop_ref[pl.ds(base + step, 1), :]
    row = lax.broadcasted_iota(jnp.int32, (SUB, SUB), 0)
    col = lax.broadcasted_iota(jnp.int32, (SUB, SUB), 1)
    causal = row >= col
    low_half = col < HEAD_SIZE
    for g in range(groups):
        sl = slice(g * lanes, (g + 1) * lanes)
        b_g = b_ref[:, g * STATE : (g + 1) * STATE]
        c_g = c_ref[:, g * STATE : (g + 1) * STATE]
        scores = jnp.where(causal, dot(c_g, b_g, ((1,), (1,))), 0.0)
        pieces = []
        for q in range(per_group // 2):
            mixes = []
            for h in (g * per_group + 2 * q, g * per_group + 2 * q + 1):
                gap = jnp.minimum(cum_cols[:, h : h + 1] - key_ref[h : h + 1, :], 100.0)
                mixes.append((scores * jnp.exp2(gap)).astype(BF16))
            pair = x_ref[:, g * lanes + q * 128 : g * lanes + (q + 1) * 128]
            none = jnp.zeros_like(pair)
            both = jnp.concatenate(
                [jnp.where(low_half, pair, none), jnp.where(low_half, none, pair)], axis=0
            )
            pieces.append(dot(jnp.concatenate(mixes, axis=1), both))
        state = state_ref[:, sl]
        out = jnp.concatenate(pieces, axis=1) + dot(c_g, state.astype(BF16)) * spread[:, sl]
        skip = jnp.concatenate(
            [
                jnp.where(low_half[:1], skip_ref[h], skip_ref[h + 1])
                for h in range(g * per_group, (g + 1) * per_group, 2)
            ],
            axis=1,
        )
        out = out + skip * x_ref[:, sl].astype(F32)
        gated = out * silu(z_ref[:, sl].astype(F32))
        mean_sq = jnp.sum(gated * gated, axis=1, keepdims=True) * (1.0 / lanes)
        normed = (gated * lax.rsqrt(mean_sq + EPSILON) * gain_ref[:, sl]).astype(BF16)

        @pl.when(step == 0)
        def _():
            top_ref[:, sl] = normed

        @pl.when(step == 1)
        def _():
            bottom_ref[:, sl] = normed

        state_ref[:, sl] = fall[:, sl] * state + fresh_ref[0, :, sl]

    next_ref[...] = state_ref[...]


def chunk_out(index, x, b, c, z, cum, key, fresh, drop, skip, gain, came, start):
    wide_x, wide_b = x.shape[1], b.shape[1]
    heads = cum.shape[0]
    base = index * (CHUNK // SUB)

    def whole(shape):
        return pl.BlockSpec(shape, lambda i: (0,) * len(shape))

    def body(*refs):
        chunk_kernel(*refs, base=base)

    return pl.pallas_call(
        body,
        grid=(CHUNK // SUB,),
        in_specs=[
            pl.BlockSpec((SUB, wide_x), lambda i: (base + i, 0)),
            pl.BlockSpec((SUB, wide_b), lambda i: (base + i, 0)),
            pl.BlockSpec((SUB, wide_b), lambda i: (base + i, 0)),
            pl.BlockSpec((SUB, wide_x), lambda i: (base + i, 0)),
            pl.BlockSpec((heads, SUB), lambda i: (0, base + i)),
            pl.BlockSpec((heads, SUB), lambda i: (0, base + i)),
            pl.BlockSpec((1, STATE, wide_x), lambda i: (base + i, 0, 0)),
            whole(drop.shape),
            pl.BlockSpec(memory_space=pltpu.SMEM),
            whole(gain.shape),
            whole(came.shape),
            whole(start.shape),
        ],
        out_specs=[whole((SUB, wide_x)), whole((SUB, wide_x)), whole((STATE, wide_x))],
        out_shape=[
            jax.ShapeDtypeStruct((SUB, wide_x), BF16),
            jax.ShapeDtypeStruct((SUB, wide_x), BF16),
            jax.ShapeDtypeStruct((STATE, wide_x), F32),
        ],
        scratch_shapes=[pltpu.VMEM((STATE, wide_x), F32)],
        name="chunk",
    )(x, b, c, z, cum, key, fresh, drop, skip, gain, came, start)


def weight_spec(cols, which):
    return pl.BlockSpec(
        (None, 16, None, 64, cols),
        lambda n, at, which=which: (at[2 * which], 0, at[2 * which + 1], 0, n),
    )


def stacked(refs):
    return jnp.concatenate([ref[...] for ref in refs], axis=0)


def rows_of(ref):
    return ref[...].reshape(ref.shape[0] * ref.shape[1], ref.shape[2])


def near_kernel(at_ref, *refs, kinds):
    per = (len(refs) - 1 - kinds) // kinds
    out_ref = refs[-1]
    total = None
    for n in range(kinds):
        term = dot(stacked(refs[n * per : (n + 1) * per]), rows_of(refs[kinds * per + n]))
        total = term if total is None else total + term
    out_ref[...] = total


def project_near(at, pieces, weight, cols=256):
    kinds = len(pieces)
    flat = [p for kind in pieces for p in kind]
    rows = sum(p.shape[0] for p in pieces[0])
    width = weight.shape[-1]

    def body(*refs):
        near_kernel(*refs, kinds=kinds)

    return pl.pallas_call(
        body,
        grid_spec=pltpu.PrefetchScalarGridSpec(
            num_scalar_prefetch=1,
            grid=(width // cols,),
            in_specs=[pl.BlockSpec(p.shape, lambda n, *_: (0, 0)) for p in flat]
            + [weight_spec(cols, n) for n in range(kinds)],
            out_specs=pl.BlockSpec((rows, cols), lambda n, *_: (0, n)),
        ),
        out_shape=jax.ShapeDtypeStruct((rows, width), F32),
        name="near",
    )(at, *flat, *([weight] * kinds))


def far_kernel(at_ref, *refs, count):
    rows = stacked(refs[:count])
    w_ref, acc_ref, out_ref = refs[count], refs[count + 1], refs[-1]
    out_ref[...] = (acc_ref[...] + dot(rows, rows_of(w_ref))).astype(BF16)


def project_far(at, pieces, weight, acc, block, before=None, cols=512):
    rows = sum(p.shape[0] for p in pieces)
    total, width = acc.shape
    extra = [] if before is None else [before]

    def body(*refs):
        far_kernel(*refs, count=len(pieces))

    return pl.pallas_call(
        body,
        grid_spec=pltpu.PrefetchScalarGridSpec(
            num_scalar_prefetch=1,
            grid=(width // cols,),
            in_specs=[pl.BlockSpec(p.shape, lambda n, *_: (0, 0)) for p in pieces]
            + [weight_spec(cols, 0), pl.BlockSpec((rows, cols), lambda n, *_: (block, n))]
            + [pl.BlockSpec(memory_space=pl.ANY)] * len(extra),
            out_specs=pl.BlockSpec((rows, cols), lambda n, *_: (block, n)),
        ),
        out_shape=jax.ShapeDtypeStruct((total, width), BF16),
        input_output_aliases={} if before is None else {len(pieces) + 3: 0},
        name="far",
    )(at, *pieces, weight, acc, *extra)


def turn(value, axis, distance):
    count = lax.axis_size(axis)
    return lax.ppermute(value, axis, [(i, (i + distance) % count) for i in range(count)])


def local(
    x_in,
    b_in,
    c_in,
    z_in,
    dt_in,
    a_log,
    skip_gain,
    norm_gain,
    conv_x,
    conv_b,
    conv_c,
    init_state,
    out_weight,
):
    tokens, wide_x = x_in.shape[1:]
    slabs = lax.axis_size("seq")
    head, part = lax.axis_index("head"), lax.axis_index("dp")
    x, b, c, z, dt = x_in[0], b_in[0], c_in[0], z_in[0], dt_in[0]
    halo = lax.ppermute(edge_rows(x, b, c), "seq", [(i, i + 1) for i in range(slabs - 1)])
    other_rows = turn(out_weight, "dp", 1)
    first = (lax.axis_index("seq") == 0).astype(jnp.int32).reshape(1)
    x, b, c, cum, key, fresh, drop, start, msg = front(
        first, x, b, c, halo, dt, a_log, conv_x, conv_b, conv_c, init_state.reshape(wide_x, STATE)
    )
    msg, other_rows = lax.optimization_barrier((msg, other_rows))
    weight = lax.all_gather(jnp.stack([out_weight, other_rows]), "seq", axis=0)
    weight = weight.reshape(2, slabs // 2, 2, *out_weight.shape)
    msg = lax.all_to_all(msg, "seq", 0, 0, tiled=True)
    came = lax.all_to_all(scan_slabs(msg), "seq", 0, 0, tiled=True)

    gain = norm_gain.reshape(1, wide_x)
    count = tokens // CHUNK
    own, ahead, behind, beyond = [], [], [], []
    for index in range(count):
        top, bottom, came = chunk_out(
            index, x, b, c, z, cum, key, fresh, drop, skip_gain, gain, came, start
        )
        own += [top, bottom]
        top_back, bottom_ahead = turn(top, "head", 1), turn(bottom, "head", -1)
        bottom_back, top_ahead = turn(bottom, "head", 1), turn(top, "head", -1)
        behind += [top_back, bottom_back]
        ahead += [top_ahead, bottom_ahead]
        beyond += [turn(top_back, "head", 1), turn(bottom_ahead, "head", -1)]

    def place(owner):
        return [owner % 2, (owner // 2 + part) % 2]

    table = [place((head + step) % 4) for step in (0, 1, 3)]
    near_at = jnp.stack([v for pair in table for v in pair]).astype(jnp.int32)
    far_at = jnp.stack(place((head + 2) % 4)).astype(jnp.int32)
    acc = project_near(near_at, (own, ahead, behind), weight)
    split = 2 * (count - 1)
    out = project_far(far_at, beyond[:split], weight, acc, 0)
    out = project_far(far_at, beyond[split:], weight, acc, count - 1, before=out)
    return out[None]


def solution(mesh):
    in_specs = (
        P("dp", "seq", "head"),
        P("dp", "seq", "head"),
        P("dp", "seq", "head"),
        P("dp", "seq", "head"),
        P("dp", "head", "seq"),
        P("head"),
        P("head"),
        P("head"),
        P(None, "head"),
        P(None, "head"),
        P(None, "head"),
        P("dp", "head", None, None),
        P(("dp", "seq"), "head"),
    )
    out_specs = P("dp", "seq", "head")

    return jax.shard_map(local, mesh=mesh, in_specs=in_specs, out_specs=out_specs, check_vma=False)
```

```python
import math

import jax
import jax.numpy as jnp
from jax import lax
from jax.experimental import pallas as pl
from jax.experimental.pallas import tpu as pltpu
from jax.sharding import PartitionSpec as P

HEAD_SIZE = 64
STATE = 128
TAPS = 4
SUB = 128
CHUNK = 256
EPSILON = 1e-05
LOG2E = math.log2(math.e)
F32 = jnp.float32
BF16 = jnp.bfloat16

LANE = 128
WIDE = 256


def in_hbm(*arrays):
    return [pltpu.with_memory_space_constraint(array, pltpu.HBM) for array in arrays]


def in_vmem(*arrays):
    return [pltpu.with_memory_space_constraint(array, pltpu.VMEM) for array in arrays]


ALL_VMEM = pl.BlockSpec(memory_space=pltpu.VMEM)


def dot(a, b, dims=((1,), (0,))):
    return lax.dot_general(a, b, (dims, ((), ())), preferred_element_type=F32)


def silu(v):
    half = 0.5 * v
    return half + half * jnp.tanh(half)


def split_two(v):
    high = v.astype(BF16)
    low = (v - high.astype(F32)).astype(BF16)
    return high, low


def head_of_lane(heads, width):
    lane = lax.broadcasted_iota(jnp.int32, (heads, width), 1)
    row = lax.broadcasted_iota(jnp.int32, (heads, width), 0)
    return lane // HEAD_SIZE == row


def widen_row(column, width):
    mask = head_of_lane(column.shape[0], width)
    return jnp.sum(jnp.where(mask, column, 0.0), axis=0, keepdims=True)


def column_of(ref, heads):
    row = lax.broadcasted_iota(jnp.int32, (heads, 1), 0)
    column = jnp.zeros((heads, 1), F32)
    for h in range(heads):
        column = jnp.where(row == h, ref[h], column)
    return column


def edge_kernel(x_ref, b_ref, c_ref, out_ref):
    wide_x, wide_b = x_ref.shape[1], b_ref.shape[1]
    out_ref[:, :wide_x] = x_ref[...]
    out_ref[:, wide_x : wide_x + wide_b] = b_ref[...]
    out_ref[:, wide_x + wide_b :] = c_ref[...]


def edge_rows(x, b, c):
    tokens, wide_x = x.shape
    wide_b = b.shape[1]
    last = tokens // 8 - 1
    return pl.pallas_call(
        edge_kernel,
        grid=(1,),
        in_specs=[
            pl.BlockSpec((8, wide_x), lambda i: (last, 0)),
            pl.BlockSpec((8, wide_b), lambda i: (last, 0)),
            pl.BlockSpec((8, wide_b), lambda i: (last, 0)),
        ],
        out_specs=pl.BlockSpec((8, wide_x + 2 * wide_b), lambda i: (0, 0)),
        out_shape=jax.ShapeDtypeStruct((8, wide_x + 2 * wide_b), BF16),
        name="edge",
    )(x, b, c)


def conv_rows(pad_ref, half_weight, rows, row, lanes):
    half = half_weight[TAPS - 1 : TAPS] * pad_ref[8 + row : 8 + row + rows, lanes]
    for back in range(1, TAPS):
        tap = TAPS - 1 - back
        half = half + half_weight[tap : tap + 1] * pad_ref[8 + row - back : 8 + row - back + rows, lanes]
    return (half + half * jnp.tanh(half)).astype(BF16)


def conv_into(raw_ref, tail_ref, weight_ref, lo, pad_ref, out_ref):
    rows, width = raw_ref.shape
    for first in range(0, width, LANE):
        sl = slice(first, first + LANE)
        at = slice(lo + first, lo + first + LANE)
        half_weight = 0.5 * weight_ref[:, sl]
        pad_ref[0:8, at] = tail_ref[:, at]
        for row in range(0, rows, SUB):
            pad_ref[8 + row : 8 + row + SUB, at] = raw_ref[row : row + SUB, sl].astype(F32)
        tail_ref[:, at] = pad_ref[rows : rows + 8, at]
        for row in range(0, rows, SUB):
            out_ref[row : row + SUB, sl] = conv_rows(pad_ref, half_weight, SUB, row, at)


def front_kernel(
    first_ref,
    x_ref,
    b_ref,
    halo_ref,
    dt_ref,
    alog_ref,
    cx_ref,
    cb_ref,
    init_ref,
    xo_ref,
    bo_ref,
    cum_ref,
    key_ref,
    drop_ref,
    start_ref,
    msg_ref,
    pad_ref,
    tail_ref,
    weight_ref,
    fall_ref,
    state_ref,
):
    step = pl.program_id(0)
    wide_x, wide_b = x_ref.shape[1], b_ref.shape[1]
    heads, tokens = dt_ref.shape
    subs = tokens // SUB
    groups = wide_b // STATE
    lanes = wide_x // groups

    @pl.when(step == 0)
    def _():
        tail_ref[...] = halo_ref[:, : wide_x + wide_b].astype(F32)
        raw = dt_ref[...]
        grown = jnp.exp(-jnp.abs(raw))
        near = 1.0 + grown
        gap = near - 1.0
        log_near = jnp.where(gap == 0.0, grown, jnp.log(near) * grown / jnp.where(gap == 0.0, 1.0, gap))
        size = jnp.maximum(raw, 0.0) + log_near
        rate = size * (-LOG2E * jnp.exp(column_of(alog_ref, heads)))
        lane = lax.broadcasted_iota(jnp.int32, (heads, SUB), 1)
        rows = []
        for j in range(subs):
            cum = rate[:, j * SUB : (j + 1) * SUB]
            shift = 1
            while shift < SUB:
                cum = cum + jnp.where(lane >= shift, pltpu.roll(cum, shift, 1), 0.0)
                shift *= 2
            size_j = size[:, j * SUB : (j + 1) * SUB]
            last = cum[:, SUB - 1 : SUB]
            cum_ref[:, j * SUB : (j + 1) * SUB] = cum
            key_ref[:, j * SUB : (j + 1) * SUB] = cum - jnp.log(size_j) * LOG2E
            weight_ref[:, j * SUB : (j + 1) * SUB] = jnp.exp2(last - cum) * size_j
            rows.append(widen_row(jnp.exp2(last), wide_x))
        rows += [jnp.ones((1, wide_x), F32)] * (8 - subs)
        fall_ref[...] = jnp.concatenate(rows, axis=0)
        reach = [jnp.ones((1, wide_x), F32)]
        for j in range(7):
            reach.append(reach[-1] * rows[j])
        drop_ref[...] = jnp.concatenate(reach, axis=0)

        @pl.when(first_ref[0] == 1)
        def _():
            for k in range(wide_x // STATE):
                state_ref[:, k * STATE : (k + 1) * STATE] = init_ref[k * STATE : (k + 1) * STATE, :].T

        @pl.when(first_ref[0] != 1)
        def _():
            state_ref[...] = jnp.zeros_like(state_ref)

    conv_into(x_ref, tail_ref, cx_ref, 0, pad_ref, xo_ref)
    conv_into(b_ref, tail_ref, cb_ref, wide_x, pad_ref, bo_ref)

    per_step = x_ref.shape[0] // SUB
    mask = head_of_lane(heads, wide_x).astype(F32).astype(BF16)
    mask = jnp.concatenate([mask, mask], axis=0)
    for k in range(per_step):
        at = pl.multiple_of(step * (per_step * SUB) + k * SUB, SUB)
        halves = jnp.concatenate(split_two(weight_ref[:, pl.ds(at, SUB)]), axis=0)
        fall = fall_ref[pl.ds(step * per_step + k, 1), :]
        for first in range(0, wide_x, WIDE):
            sl = slice(first, first + WIDE)
            g = first // lanes
            spread = dot(halves, mask[:, sl], ((0,), (0,)))
            inner = (spread * xo_ref[k * SUB : (k + 1) * SUB, sl].astype(F32)).astype(BF16)
            fresh = dot(
                bo_ref[k * SUB : (k + 1) * SUB, g * STATE : (g + 1) * STATE], inner, ((0,), (0,))
            )
            before = state_ref[:, sl]
            start_ref[k, :, sl] = before.astype(BF16)
            state_ref[:, sl] = fall[:, sl] * before + fresh

    @pl.when(step == pl.num_programs(0) - 1)
    def _():
        tiles = STATE // 8
        whole = drop_ref[subs : subs + 1, :]
        high = whole.astype(BF16).astype(F32)
        low = whole - high
        for g in range(groups):
            own = state_ref[:, g * lanes : (g + 1) * lanes].reshape(tiles, 8, lanes)
            msg_ref[g * tiles : (g + 1) * tiles, :, :lanes] = own.astype(BF16)
            pieces = [
                part[:, g * lanes + q * 128 : g * lanes + (q + 1) * 128]
                for part in (high, low)
                for q in range(lanes // 128)
            ]
            tile = jnp.concatenate(pieces, axis=0)
            msg_ref[g * tiles : (g + 1) * tiles, :, lanes:] = jnp.broadcast_to(
                tile[None], (tiles, 8, 128)
            ).astype(BF16)


def front(first, x, b, halo, dt, a_log, conv_x, conv_b, init):
    tokens, wide_x = x.shape
    wide_b = b.shape[1]
    heads = dt.shape[0]
    subs = tokens // SUB
    groups = wide_b // STATE
    lanes = wide_x // groups
    parts = groups * STATE // 8
    per_step = CHUNK // SUB

    def whole(*shape):
        return pl.BlockSpec(shape, lambda i, *_: (0,) * len(shape))

    return pl.pallas_call(
        front_kernel,
        grid_spec=pltpu.PrefetchScalarGridSpec(
            num_scalar_prefetch=1,
            grid=(tokens // CHUNK,),
            in_specs=[
                pl.BlockSpec((CHUNK, wide_x), lambda i, *_: (i, 0)),
                pl.BlockSpec((CHUNK, wide_b), lambda i, *_: (i, 0)),
                ALL_VMEM,
                whole(heads, tokens),
                pl.BlockSpec(memory_space=pltpu.SMEM),
                whole(TAPS, wide_x),
                whole(TAPS, wide_b),
                whole(wide_x, STATE),
            ],
            out_specs=[
                pl.BlockSpec((CHUNK, wide_x), lambda i, *_: (i, 0)),
                pl.BlockSpec((CHUNK, wide_b), lambda i, *_: (i, 0)),
                whole(heads, tokens),
                whole(heads, tokens),
                whole(8, wide_x),
                pl.BlockSpec((per_step, STATE, wide_x), lambda i, *_: (i, 0, 0)),
                whole(parts, 8, lanes + 128),
            ],
            scratch_shapes=[
                pltpu.VMEM((CHUNK + 8, wide_x + wide_b), F32),
                pltpu.VMEM((8, wide_x + wide_b), F32),
                pltpu.VMEM((heads, tokens), F32),
                pltpu.VMEM((8, wide_x), F32),
                pltpu.VMEM((STATE, wide_x), F32),
            ],
        ),
        out_shape=[
            jax.ShapeDtypeStruct((tokens, wide_x), BF16),
            jax.ShapeDtypeStruct((tokens, wide_b), BF16),
            jax.ShapeDtypeStruct((heads, tokens), F32),
            jax.ShapeDtypeStruct((heads, tokens), F32),
            jax.ShapeDtypeStruct((8, wide_x), F32),
            jax.ShapeDtypeStruct((subs, STATE, wide_x), BF16),
            jax.ShapeDtypeStruct((parts, 8, lanes + 128), BF16),
        ],
        name="front",
    )(first, *in_hbm(x, b), *in_vmem(halo), *in_hbm(dt), a_log, *in_hbm(conv_x, conv_b, init))


def scan_kernel(msg_ref, out_ref):
    slabs, _, wide = msg_ref.shape
    lanes = wide - 128
    pieces = lanes // 128
    running = [jnp.zeros((8, 128), F32) for _ in range(pieces)]
    for s in range(slabs):
        falls = msg_ref[s, :, lanes:].astype(F32)
        for q in range(pieces):
            out_ref[s, :, q * 128 : (q + 1) * 128] = running[q].astype(BF16)
            fall = falls[q : q + 1, :] + falls[pieces + q : pieces + q + 1, :]
            running[q] = fall * running[q] + msg_ref[s, :, q * 128 : (q + 1) * 128].astype(F32)


def scan_slabs(msg):
    slabs, _, wide = msg.shape
    return pl.pallas_call(
        scan_kernel,
        in_specs=[ALL_VMEM],
        out_shape=jax.ShapeDtypeStruct((slabs, 8, wide - 128), BF16),
        name="scan",
    )(*in_vmem(msg))


def mid_kernel(
    x_ref, b_ref, c_ref, prev_ref, halo_ref, cum_ref, key_ref, cc_ref, skip_ref, out_ref, co_ref, pad_ref, *, base
):
    wide_x, wide_b = x_ref.shape[1], b_ref.shape[1]
    groups = wide_b // STATE
    lanes = wide_x // groups
    per_group = cum_ref.shape[0] // groups
    start = (pl.program_id(0) == 0) & (base == 0)
    halo = halo_ref[:, wide_x + wide_b :]
    before = jnp.where(start, halo.astype(F32), prev_ref[...].astype(F32))
    pad_ref[0:8] = before
    pad_ref[8:] = c_ref[...].astype(F32)
    co_ref[...] = conv_rows(pad_ref, 0.5 * cc_ref[...], SUB, 0, slice(None))

    cum_cols = cum_ref[...].T
    row = lax.broadcasted_iota(jnp.int32, (SUB, SUB), 0)
    col = lax.broadcasted_iota(jnp.int32, (SUB, SUB), 1)
    causal = row >= col
    low_half = col < HEAD_SIZE
    for g in range(groups):
        part = slice(g * STATE, (g + 1) * STATE)
        scores = jnp.where(causal, dot(co_ref[:, part], b_ref[:, part], ((1,), (1,))), 0.0)
        for q in range(lanes // LANE):
            sl = slice(g * lanes + q * LANE, g * lanes + (q + 1) * LANE)
            head = g * per_group + 2 * q
            mixes = []
            for h in (head, head + 1):
                gap = jnp.minimum(cum_cols[:, h : h + 1] - key_ref[h : h + 1, :], 100.0)
                mixes.append((scores * jnp.exp2(gap)).astype(BF16))
            pair = x_ref[:, sl]
            none = jnp.zeros_like(pair)
            both = jnp.concatenate(
                [jnp.where(low_half, pair, none), jnp.where(low_half, none, pair)], axis=0
            )
            skip = jnp.where(low_half[:1], skip_ref[head], skip_ref[head + 1])
            out_ref[:, sl] = dot(jnp.concatenate(mixes, axis=1), both) + skip * pair.astype(F32)


def mid(base, blocks, x, b, c, halo, cum, key, conv_c, skip):
    wide_x, wide_b = x.shape[1], b.shape[1]
    heads = cum.shape[0]
    per = SUB // 8

    def body(*refs):
        mid_kernel(*refs, base=base)

    return pl.pallas_call(
        body,
        grid=(blocks,),
        in_specs=[
            pl.BlockSpec((SUB, wide_x), lambda i: (base + i, 0)),
            pl.BlockSpec((SUB, wide_b), lambda i: (base + i, 0)),
            pl.BlockSpec((SUB, wide_b), lambda i: (base + i, 0)),
            pl.BlockSpec((8, wide_b), lambda i: (jnp.maximum(per * (base + i), 1) - 1, 0)),
            ALL_VMEM,
            pl.BlockSpec((heads, SUB), lambda i: (0, base + i)),
            pl.BlockSpec((heads, SUB), lambda i: (0, base + i)),
            pl.BlockSpec(conv_c.shape, lambda i: (0, 0)),
            pl.BlockSpec(memory_space=pltpu.SMEM),
        ],
        out_specs=[
            pl.BlockSpec((SUB, wide_x), lambda i: (i, 0)),
            pl.BlockSpec((SUB, wide_b), lambda i: (i, 0)),
        ],
        out_shape=[
            jax.ShapeDtypeStruct((blocks * SUB, wide_x), F32),
            jax.ShapeDtypeStruct((blocks * SUB, wide_b), BF16),
        ],
        scratch_shapes=[pltpu.VMEM((SUB + 8, wide_b), F32)],
        name="mid",
    )(*in_hbm(x, b, c, c), *in_vmem(halo), *in_hbm(cum, key, conv_c), skip)


def block_kernel(
    y_ref, c_ref, z_ref, cum_ref, drop_ref, start_ref, gain_ref, came_ref, out_ref, gated_ref, *, index
):
    wide_x, wide_b = y_ref.shape[1], c_ref.shape[1]
    groups = wide_b // STATE
    lanes = wide_x // groups
    tiles = STATE // 8
    halves = jnp.concatenate(split_two(jnp.exp2(cum_ref[...])), axis=0)
    mask = head_of_lane(cum_ref.shape[0], wide_x).astype(F32).astype(BF16)
    mask = jnp.concatenate([mask, mask], axis=0)
    for g in range(groups):
        c_g = c_ref[:, g * STATE : (g + 1) * STATE]
        square = None
        for at in range(0, lanes, WIDE):
            sl = slice(g * lanes + at, g * lanes + at + WIDE)
            came = came_ref[g * tiles : (g + 1) * tiles, :, at : at + WIDE]
            came = came.astype(F32).reshape(STATE, WIDE)
            state = drop_ref[index : index + 1, sl] * came + start_ref[:, sl].astype(F32)
            spread = dot(halves, mask[:, sl], ((0,), (0,)))
            out = y_ref[:, sl] + dot(c_g, state.astype(BF16)) * spread
            gated = out * silu(z_ref[:, sl].astype(F32))
            gated_ref[:, at : at + WIDE] = gated
            term = gated[:, :LANE] * gated[:, :LANE] + gated[:, LANE:] * gated[:, LANE:]
            square = term if square is None else square + term
        mean_sq = jnp.sum(square, axis=1, keepdims=True) * (1.0 / lanes)
        scale = lax.rsqrt(mean_sq + EPSILON)
        for at in range(0, lanes, LANE):
            sl = slice(g * lanes + at, g * lanes + at + LANE)
            out_ref[:, sl] = (gated_ref[:, at : at + LANE] * scale * gain_ref[:, sl]).astype(BF16)


def block_out(index, local_index, y, c, z, cum, drop, start, gain, came):
    wide_x, wide_b = y.shape[1], c.shape[1]
    heads = cum.shape[0]

    def body(*refs):
        block_kernel(*refs, index=index)

    return pl.pallas_call(
        body,
        grid=(1,),
        in_specs=[
            pl.BlockSpec((SUB, wide_x), lambda i: (local_index, 0)),
            pl.BlockSpec((SUB, wide_b), lambda i: (local_index, 0)),
            pl.BlockSpec((SUB, wide_x), lambda i: (index, 0)),
            pl.BlockSpec((heads, SUB), lambda i: (0, index)),
            pl.BlockSpec(drop.shape, lambda i: (0, 0)),
            pl.BlockSpec((None, STATE, wide_x), lambda i: (index, 0, 0)),
            pl.BlockSpec(gain.shape, lambda i: (0, 0)),
            ALL_VMEM,
        ],
        out_specs=pl.BlockSpec((SUB, wide_x), lambda i: (0, 0)),
        out_shape=jax.ShapeDtypeStruct((SUB, wide_x), BF16),
        scratch_shapes=[pltpu.VMEM((SUB, wide_x * STATE // wide_b), F32)],
        name="block",
    )(*in_hbm(y, c, z, cum, drop, start, gain), *in_vmem(came))


def weight_spec(cols, which):
    return pl.BlockSpec(
        (None, 16, None, 64, cols),
        lambda n, at, which=which: (at[2 * which], 0, at[2 * which + 1], 0, n),
    )


def stacked(refs):
    return jnp.concatenate([ref[...] for ref in refs], axis=0)


def rows_of(ref):
    return ref[...].reshape(ref.shape[0] * ref.shape[1], ref.shape[2])


def project(at, kinds, pieces, weight, acc=None, cols=512):
    flat = [p for kind in pieces for p in kind]
    per, count = len(pieces[0]), len(kinds)
    rows = sum(p.shape[0] for p in pieces[0])
    width = weight.shape[-1]
    tile = pl.BlockSpec((rows, cols), lambda n, *_: (0, n))
    operands = [*flat, *([weight] * count)]
    specs = [ALL_VMEM for _ in flat]
    specs += [weight_spec(cols, kind) for kind in kinds]
    if acc is not None:
        operands.append(acc)
        specs.append(tile)

    def body(at_ref, *refs):
        weights = refs[count * per : count * per + count]
        total = None if acc is None else refs[count * per + count][...].astype(F32)
        for n in range(count):
            term = dot(stacked(refs[n * per : (n + 1) * per]), rows_of(weights[n]))
            total = term if total is None else total + term
        refs[-1][...] = total.astype(BF16)

    return pl.pallas_call(
        body,
        grid_spec=pltpu.PrefetchScalarGridSpec(
            num_scalar_prefetch=1, grid=(width // cols,), in_specs=specs, out_specs=tile
        ),
        out_shape=jax.ShapeDtypeStruct((rows, width), BF16),
        compiler_params=pltpu.CompilerParams(vmem_limit_bytes=32 * 2**20),
        name="project",
    )(at, *in_vmem(*flat), *in_hbm(*operands[len(flat) :]))


def turn(value, axis, distance):
    count = lax.axis_size(axis)
    return lax.ppermute(value, axis, [(i, (i + distance) % count) for i in range(count)])


def local(
    x_in,
    b_in,
    c_in,
    z_in,
    dt_in,
    a_log,
    skip_gain,
    norm_gain,
    conv_x,
    conv_b,
    conv_c,
    init_state,
    out_weight,
):
    tokens, wide_x = x_in.shape[1:]
    slabs = lax.axis_size("seq")
    head, part = lax.axis_index("head"), lax.axis_index("dp")
    x, b, c, z, dt = x_in[0], b_in[0], c_in[0], z_in[0], dt_in[0]
    halo = lax.ppermute(edge_rows(x, b, c), "seq", [(i, i + 1) for i in range(slabs - 1)])
    first = (lax.axis_index("seq") == 0).astype(jnp.int32).reshape(1)
    x, b, cum, key, drop, start, msg = front(
        first, x, b, halo, dt, a_log, conv_x, conv_b, init_state.reshape(wide_x, STATE)
    )
    count = tokens // SUB
    msg = lax.all_to_all(msg, "seq", 0, 0, tiled=True)
    other_rows = turn(out_weight, "dp", 1)
    came = lax.all_to_all(scan_slabs(msg), "seq", 0, 0, tiled=True)
    half = count // 2
    parts = [mid(0, half, x, b, c, halo, cum, key, conv_c, skip_gain)]
    parts.append(mid(half, count - half, x, b, c, halo, cum, key, conv_c, skip_gain))

    gain = norm_gain.reshape(1, wide_x)
    own, ahead, behind, beyond = [], [], [], []
    for index in range(count):
        y, c_out = parts[index // half]
        rows = block_out(index, index % half, y, c_out, z, cum, drop, start, gain, came)
        if index == 0:
            rows, other_rows = lax.optimization_barrier((rows, other_rows))
        own.append(rows)
        behind.append(turn(rows, "head", 1))
        ahead.append(turn(rows, "head", -1))
        beyond.append(
            turn(behind[-1], "head", 1) if index % 2 == 0 else turn(ahead[-1], "head", -1)
        )

    def place(owner):
        return [owner % 2, (owner // 2 + part) % 2]

    weight = lax.all_gather(jnp.stack([out_weight, other_rows]), "seq", axis=0)
    weight = weight.reshape(2, slabs // 2, 2, *out_weight.shape)
    at = jnp.stack([v for step in range(4) for v in place((head + step) % 4)]).astype(jnp.int32)
    acc = project(at, (0, 1, 3), [own, ahead, behind], weight, cols=1024)
    out = project(at, (2,), [beyond], weight, acc=acc, cols=1024)
    return out[None]


def solution(mesh):
    in_specs = (
        P("dp", "seq", "head"),
        P("dp", "seq", "head"),
        P("dp", "seq", "head"),
        P("dp", "seq", "head"),
        P("dp", "head", "seq"),
        P("head"),
        P("head"),
        P("head"),
        P(None, "head"),
        P(None, "head"),
        P(None, "head"),
        P("dp", "head", None, None),
        P(("dp", "seq"), "head"),
    )
    out_specs = P("dp", "seq", "head")

    return jax.shard_map(local, mesh=mesh, in_specs=in_specs, out_specs=out_specs, check_vma=False)
```
